256 devices in a mesh: rec: 32 (over x, z), head: 8 (over y, core).
Axes of the slice: x: 4, y: 4, z: 8, core: 2. Of those that a mesh axis runs over, the one named last changes fastest.
Arguments:
- spectrogram: bfloat16 [32, 1536, 8192], P('rec', 'head'), may hold values from -8 to 8
- epoch_counts: int32 [32], P('rec'), may hold values from 1 to 1536, as said below
- conv_first: bfloat16 [7, 64, 256], replicated, may hold values from -0.25 to 0.25
- bias_first: float32 [256], replicated, may hold values from -3 to 3
- conv_second: bfloat16 [7, 256, 1024], replicated, may hold values from -0.125 to 0.125
- bias_second: float32 [1024], replicated, may hold values from -3 to 3
- projection: bfloat16 [1024, 3, 1024], replicated
Outputs:
- attended: bfloat16 [32, 1536, 1024], P('rec', None, 'head')
The draws below stay inside these ranges and needn't reach their ends.
Inputs may be any that keep to these rules, and one draw needn't show every extreme that they name: Recording r has valid epochs in slots 0 to epoch_counts[r] - 1; some recording fills all 1536 slots.
All inputs are finite; a program needn't handle non-finite values.
Results may differ from the reference program's by a relative error of at most 0.018.
Values may be sent and summed in bfloat16 or wider, within the bound.
A program may use at most 64 MiB of HBM per device.

```python
import math
import jax
import jax.numpy as jnp
from jax import lax

FRAMES = 128
C0 = 64
C1 = 256
D = 1024
HEADS = 16
HD = 64
KERNEL = 7
RECS = 32
CAP = 1536


def draw_epoch_counts(key, part):
    key_drawn, key_busy = jax.random.split(key)
    typical = jax.random.randint(key_drawn, (RECS,), 1, 2 * CAP // 3 + 1, dtype=jnp.int32)
    busiest = jax.random.randint(key_busy, (), 0, RECS, dtype=jnp.int32)
    return jnp.where(jnp.arange(RECS, dtype=jnp.int32) == busiest, CAP, typical).astype(jnp.int32)


def draw_spectrogram(key, part):
    key_level, key_noise = jax.random.split(jax.random.fold_in(key, 11))
    level = 1.5 * jax.random.normal(key_level, (RECS, CAP, 1, C0), jnp.float32)
    noise = jax.random.normal(key_noise, (RECS, CAP, FRAMES, C0), jnp.float32)
    field = jnp.clip(level + noise, -8.0, 8.0)
    return field.reshape(RECS, CAP, FRAMES * C0).astype(jnp.bfloat16)


def draw_projection(key, part):
    key_base = jax.random.fold_in(key, 0)
    standard = jax.random.normal(key_base, (D, 3, D), jnp.float32) / math.sqrt(D)
    return jnp.stack([1.5 * standard[:, 0], 1.5 * standard[:, 1], standard[:, 2]], axis=1).astype(jnp.bfloat16)


def normal_values(own_key, extent, deviation, limit, kind=jnp.bfloat16):
    values = deviation * jax.random.normal(own_key, extent, jnp.float32)
    return jnp.clip(values, min=-limit, max=limit).astype(kind)


def setup_inputs(seed: int = 0) -> dict:
    key_list = jax.random.split(jax.random.key(seed), 8)
    spectrogram = draw_spectrogram(jax.random.fold_in(key_list[7], 71), 0)
    epoch_counts = draw_epoch_counts(jax.random.fold_in(key_list[7], 71), 0)
    conv_first = normal_values(key_list[2], (KERNEL, C0, C1), (KERNEL * C0) ** -0.5, 0.25)
    bias_first = normal_values(key_list[3], (C1,), 0.5, 3.0, jnp.float32)
    conv_second = normal_values(key_list[4], (KERNEL, C1, D), (KERNEL * C1) ** -0.5, 0.125)
    bias_second = normal_values(key_list[5], (D,), 0.5, 3.0, jnp.float32)
    projection = draw_projection(jax.random.fold_in(key_list[7], 71), 0)
    return {"spectrogram": spectrogram, "epoch_counts": epoch_counts, "conv_first": conv_first, "bias_first": bias_first, "conv_second": conv_second, "bias_second": bias_second, "projection": projection}


def conv_layer(inputs, weight, biases):
    number, length, channels = inputs.shape
    kernel_len = weight.shape[0]
    padded = jnp.pad(inputs, ((0, 0), (kernel_len // 2, kernel_len // 2), (0, 0)))
    columns = jnp.stack([padded[:, offset:offset + length:2, :] for offset in range(kernel_len)], axis=2)
    columns = columns.reshape(number * (length // 2), kernel_len * channels)
    result = jnp.dot(columns, weight.reshape(kernel_len * channels, weight.shape[2]), preferred_element_type=jnp.float32) + biases
    return result.reshape(number, length // 2, weight.shape[2])


def embed_block(tile_rows, conv_first, bias_first, conv_second, bias_second):
    epochs_here = tile_rows.shape[0]
    channels = conv_first.shape[1]
    spectra = tile_rows.reshape(epochs_here, tile_rows.shape[1] // channels, channels)
    hidden = jax.nn.gelu(conv_layer(spectra, conv_first, bias_first)).astype(jnp.bfloat16)
    deeper = jax.nn.gelu(conv_layer(hidden, conv_second, bias_second))
    return jnp.mean(deeper, axis=1).astype(jnp.bfloat16)


def reference(spectrogram, epoch_counts, conv_first, bias_first, conv_second, bias_second, projection):
    def one_recording(recording):
        epoch_rows, recorded = recording
        embedded = embed_block(epoch_rows, conv_first, bias_first, conv_second, bias_second)
        mixed_rows = jnp.dot(embedded, projection.reshape(D, 3 * D), preferred_element_type=jnp.float32).astype(jnp.bfloat16)
        mixed_rows = mixed_rows.reshape(CAP, 3, HEADS, HD).astype(jnp.float32)
        key_live = jnp.arange(CAP) < recorded
        scores = jnp.einsum("qhd,khd->hqk", mixed_rows[:, 0], mixed_rows[:, 1]) * (HD ** -0.5)
        scores = jnp.where(key_live[None, None, :], scores, -1e30)
        row_max = jnp.max(scores, axis=-1, keepdims=True)
        powered = jnp.exp(scores - row_max)
        probabilities = (powered / jnp.sum(powered, axis=-1, keepdims=True)).astype(jnp.bfloat16)
        attended = jnp.einsum("hqk,khd->qhd", probabilities.astype(jnp.float32), mixed_rows[:, 2])
        attended = jnp.where(key_live[:, None, None], attended, jnp.zeros_like(attended))
        return attended.reshape(CAP, D).astype(jnp.bfloat16)

    return lax.map(one_recording, (spectrogram, epoch_counts))
```

```python
import functools

import jax
import jax.numpy as jnp
from jax import lax
from jax.experimental import pallas as pl
from jax.experimental.pallas import tpu as pltpu
from jax.sharding import PartitionSpec as P

HD = 64
ROOT = 0.7978845608028654
CUBE = ROOT * 0.044715
GROUP = 4


def gelu_twice(y):
    return y + y * jnp.tanh(y * (ROOT + CUBE * (y * y)))


def embed_kernel(x_ref, w1_ref, b1_ref, w2_ref, b2_ref, o_ref, h_ref, acc_ref, w1p_ref):
    rows = x_ref.shape[0]
    taps, c0, c1 = w1_ref.shape
    wide = (taps + 1) * c0
    frames = x_ref.shape[1] // (2 * c0)
    lane = 2 * c0
    w1p_ref[0:c0, :] = jnp.zeros((c0, c1), jnp.bfloat16)
    w1p_ref[c0:wide, :] = w1_ref[...].reshape(taps * c0, c1)
    blank = jnp.zeros((rows, c1), jnp.bfloat16)
    for t in (0, 1, 2, frames + 3, frames + 4, frames + 5):
        h_ref[t] = blank
    bias = b1_ref[...]

    def first(t, lhs, weight):
        y = jnp.dot(lhs, weight, preferred_element_type=jnp.float32) + bias
        h_ref[t + 3] = (0.5 * gelu_twice(y)).astype(jnp.bfloat16)

    first(0, x_ref[:, 0 : 2 * lane], w1p_ref[2 * lane : 4 * lane, :])
    first(1, x_ref[:, 0 : 3 * lane], w1p_ref[lane : 4 * lane, :])
    first(frames - 1, x_ref[:, (frames - 3) * lane : frames * lane], w1p_ref[0 : 3 * lane, :])

    def first_step(i, _):
        start = pl.multiple_of(i * lane, lane)
        first(i + 2, x_ref[:, pl.ds(start, wide)], w1p_ref[...])
        return 0

    lax.fori_loop(0, frames - 3, first_step, 0)
    acc_ref[...] = jnp.zeros_like(acc_ref)
    half = frames // 2

    def second_step(i, _):
        for n in range(acc_ref.shape[1] // c1):
            cols = slice(n * c1, (n + 1) * c1)
            lhs = jnp.concatenate(
                [
                    jnp.concatenate([h_ref[2 * (i * GROUP + g) + k] for k in range(taps)], axis=1)
                    for g in range(GROUP)
                ],
                axis=0,
            )
            y = jnp.dot(lhs, w2_ref[:, cols], preferred_element_type=jnp.float32) + b2_ref[:, cols]
            y = gelu_twice(y)
            total = y[0:rows]
            for g in range(1, GROUP):
                total = total + y[g * rows : (g + 1) * rows]
            acc_ref[:, cols] += total
        return 0

    lax.fori_loop(0, half // GROUP, second_step, 0)
    o_ref[...] = (acc_ref[...] * (0.5 / half)).astype(jnp.bfloat16)


def embed(x, w1, b1, w2, b2):
    rows = x.shape[0]
    taps, c0, c1 = w1.shape
    width = w2.shape[2]
    frames = x.shape[1] // (2 * c0)
    return pl.pallas_call(
        embed_kernel,
        out_shape=jax.ShapeDtypeStruct((rows, width), jnp.bfloat16),
        scratch_shapes=[
            pltpu.VMEM((frames + 6, rows, c1), jnp.bfloat16),
            pltpu.VMEM((rows, width), jnp.float32),
            pltpu.VMEM(((taps + 1) * c0, c1), jnp.bfloat16),
        ],
        compiler_params=pltpu.CompilerParams(vmem_limit_bytes=48 * 1024 * 1024),
        name="embed",
    )(x, w1, b1.reshape(1, -1), w2.reshape(taps * c1, width), b2.reshape(1, -1))


def shards(spectrogram, epoch_counts, conv_first, bias_first, conv_second, bias_second, projection):
    recorded = epoch_counts[0]
    embedded = embed(spectrogram[0], conv_first, bias_first, conv_second, bias_second)
    slot_count = embedded.shape[0]
    heads_dev = lax.axis_size("head")
    model_width = projection.shape[0]
    group_width = model_width // heads_dev
    mixed_rows = jnp.dot(
        embedded,
        projection.reshape(model_width, 3 * model_width),
        preferred_element_type=jnp.float32,
    ).astype(jnp.bfloat16)
    mixed_rows = mixed_rows.reshape(slot_count, 3, heads_dev, group_width)
    regrouped = lax.all_to_all(mixed_rows, "head", split_axis=2, concat_axis=0, tiled=True)
    regrouped = regrouped.reshape(slot_count * heads_dev, 3, group_width)
    epoch_total = regrouped.shape[0]
    heads_here = group_width // HD
    queries = regrouped[:, 0].reshape(epoch_total, heads_here, HD)
    key_rows = regrouped[:, 1].reshape(epoch_total, heads_here, HD)
    values = regrouped[:, 2].reshape(epoch_total, heads_here, HD)
    key_live = jnp.arange(epoch_total, dtype=jnp.int32) < recorded
    scores = jnp.einsum(
        "qhd,khd->hqk", queries, key_rows, preferred_element_type=jnp.float32
    ) * HD ** (-0.5)
    scores = jnp.where(key_live[None, None, :], scores, -1e30)
    row_max = jnp.max(scores, axis=-1, keepdims=True)
    powered = jnp.exp(scores - row_max)
    probabilities = (powered / jnp.sum(powered, axis=-1, keepdims=True)).astype(jnp.bfloat16)
    attended = jnp.einsum("hqk,khd->qhd", probabilities, values, preferred_element_type=jnp.float32)
    attended = jnp.where(key_live[:, None, None], attended, jnp.zeros_like(attended))
    return attended.reshape(1, epoch_total, group_width).astype(jnp.bfloat16)


def solution(mesh):
    return jax.shard_map(
        shards,
        mesh=mesh,
        in_specs=(P("rec", "head", None), P("rec"), P(), P(), P(), P(), P()),
        out_specs=P("rec", None, "head"),
        check_vma=False,
    )
```

```python
import functools

import jax
import jax.numpy as jnp
from jax import lax
from jax.experimental import pallas as pl
from jax.experimental.pallas import tpu as pltpu
from jax.sharding import PartitionSpec as P

HD = 64
ROOT = 0.7978845608028654
CUBE = ROOT * 0.044715
LOG2E = 1.4426950408889634
CHUNKS = 2
FRAMES_STEP = 8
PAIRS_STEP = 8
Q_ROWS = 256
F32 = jnp.float32
BF16 = jnp.bfloat16


def gelu_twice(y):
    return y + y * jnp.tanh(y * (ROOT + CUBE * (y * y)))


def dot(a, b):
    return jnp.dot(a, b, preferred_element_type=F32)


def first_layer(x_ref, rows, n, bias, w1p_ref, x0_ref, x1_ref, x2_ref, x3_ref, carry_ref):
    c1 = w1p_ref.shape[1]
    lane = w1p_ref.shape[0] // 4
    frames = x_ref.shape[1] // lane
    blank = jnp.zeros((n, c1), BF16)
    x0_ref[0, :, c1:] = blank
    x1_ref[0, :, c1:] = blank
    carry_ref[...] = jnp.zeros_like(carry_ref)

    def emit(p, even0, odd0, even1, odd1):
        before1, before0, odd_before = carry_ref[0], carry_ref[1], carry_ref[2]
        x0_ref[p, :, :c1] = (before1 - even1).astype(BF16)
        x1_ref[p, :, :c1] = (even0 + even1).astype(BF16)
        x2_ref[p] = (even1 - even0).astype(BF16)
        x3_ref[p, :, :c1] = (before0 - even0).astype(BF16)
        x0_ref[p + 1, :, c1:] = (odd0 - odd1).astype(BF16)
        x1_ref[p + 1, :, c1:] = odd1.astype(BF16)
        x3_ref[p, :, c1:] = (odd_before - odd0).astype(BF16)
        carry_ref[0] = even1
        carry_ref[1] = even0
        carry_ref[2] = odd1

    def act(y):
        return 0.5 * gelu_twice(y + bias)

    def piece(t):
        lo, hi = max(t - 2, 0), min(t + 2, frames)
        weight = w1p_ref[(lo - t + 2) * lane : (hi - t + 2) * lane, :]
        return act(dot(x_ref[rows, lo * lane : hi * lane], weight))

    def window(t):
        return x_ref[rows, pl.ds(pl.multiple_of((t - 2) * lane, lane), 4 * lane)]

    def many(p, count):
        lhs = jnp.concatenate([window(4 * p + j) for j in range(4 * count)], axis=0)
        y = act(dot(lhs, w1p_ref[...]))
        for q in range(count):
            emit(p + q, *[y[(4 * q + j) * n : (4 * q + j + 1) * n] for j in range(4)])

    per = FRAMES_STEP // 4
    quads = frames // 4
    emit(0, *[piece(j) for j in range(4)])

    def step(i, _):
        many(1 + i * per, per)
        return 0

    loops = (quads - 2) // per
    lax.fori_loop(0, loops, step, 0)
    for p in range(1 + loops * per, quads - 1):
        many(p, 1)
    emit(quads - 1, *[piece(frames - 4 + j) for j in range(4)])
    x3_ref[quads, :, :c1] = carry_ref[1].astype(BF16)
    x3_ref[quads, :, c1:] = carry_ref[2].astype(BF16)


def second_layer(n, bias_ref, wt_ref, x0_ref, x1_ref, x2_ref, x3_ref, part_ref, acc_ref):
    c1 = x2_ref.shape[2]
    width = wt_ref.shape[1]
    acc_ref[...] = jnp.zeros_like(acc_ref)

    def step(i, _):
        def rows_of(make):
            return jnp.concatenate([make(i * PAIRS_STEP + g) for g in range(PAIRS_STEP)], axis=0)

        lhs0 = rows_of(lambda p: jnp.concatenate([x0_ref[p], x0_ref[p + 1, :, c1:]], axis=1))
        lhs1 = rows_of(lambda p: jnp.concatenate([x1_ref[p], x1_ref[p + 1, :, c1:]], axis=1))
        lhs2 = rows_of(lambda p: x2_ref[p])
        lhs3 = rows_of(
            lambda p: jnp.concatenate(
                [x3_ref[p + 1, :, :c1], x3_ref[p, :, c1:], x3_ref[p + 1, :, c1:]], axis=1
            )
        )
        for block in range(width // c1):
            cols = slice(block * c1, (block + 1) * c1)
            slot = (block % 2) * 2
            part_ref[slot] = dot(lhs1, wt_ref[3 * c1 : 6 * c1, cols]) + bias_ref[:, cols]
            part_ref[slot + 1] = dot(lhs2, wt_ref[6 * c1 : 7 * c1, cols])
            y0 = dot(lhs0, wt_ref[0 : 3 * c1, cols]) + (part_ref[slot] + part_ref[slot + 1])
            y1 = (part_ref[slot] - part_ref[slot + 1]) - dot(lhs3, wt_ref[7 * c1 : 10 * c1, cols])
            y = gelu_twice(y0) + gelu_twice(y1)
            total = y[0:n]
            for g in range(1, PAIRS_STEP):
                total = total + y[g * n : (g + 1) * n]
            acc_ref[:, cols] += total
        return 0

    lax.fori_loop(0, x2_ref.shape[0] // PAIRS_STEP, step, 0)


def attend(count, q_ref, k_ref, v_ref, o_ref):
    slots, width = k_ref.shape
    k_row = lax.broadcasted_iota(jnp.int32, (slots, width), 0)
    k_lane = lax.broadcasted_iota(jnp.int32, (slots, width), 1)
    q_lane = lax.broadcasted_iota(jnp.int32, (Q_ROWS, width), 1)
    keys, values = [], []
    zero = jnp.zeros((), F32)
    for head in range(2):
        mine = (k_lane >= head * HD) & (k_lane < (head + 1) * HD)
        spare = k_lane == (HD if head == 0 else 0)
        bias = jnp.where(k_row < count, zero, F32(-1e30))
        keys.append(jnp.where(mine, k_ref[...].astype(F32), jnp.where(spare, bias, zero)).astype(BF16))
        values.append(
            jnp.where(mine, v_ref[...].astype(F32), jnp.where(spare, F32(1), zero)).astype(BF16)
        )

    for block in range(slots // Q_ROWS):
        rows = slice(block * Q_ROWS, (block + 1) * Q_ROWS)
        query = q_ref[rows, :].astype(F32)
        outs = []
        for head in range(2):
            mine = (q_lane >= head * HD) & (q_lane < (head + 1) * HD)
            at = HD if head == 0 else 0
            wide = jnp.where(mine, query, jnp.where(q_lane == at, F32(1), zero)).astype(BF16)
            scores = lax.dot_general(
                wide, keys[head], (((1,), (1,)), ((), ())), preferred_element_type=F32
            )
            top = jnp.max(scores, axis=1, keepdims=True)
            powered = jnp.exp2(scores - top).astype(BF16)
            summed = dot(powered, values[head])
            outs.append(summed / summed[:, at : at + 1])
        row = lax.broadcasted_iota(jnp.int32, (Q_ROWS, width), 0) + block * Q_ROWS
        out = jnp.where(q_lane < HD, outs[0], outs[1])
        o_ref[rows, :] = jnp.where(row < count, out, zero).astype(BF16)


def body(
    ring,
    count_ref, x_hbm, w1_ref, b1_ref, w2_hbm, b2_ref, proj_hbm,
    o_ref,
    x_ref, w1p_ref, wt_ref, mid_ref, proj_ref,
    x0_ref, x1_ref, x2_ref, x3_ref, carry_ref, part_ref, acc_ref,
    send_ref, got_ref,
    x_sem, w_sem, p_sem, send_sem, recv_sem,
):
    me = lax.axis_index("head")
    rec = lax.axis_index("rec")
    total_rows = x_ref.shape[0]
    n = total_rows // CHUNKS
    taps, c0, c1 = w1_ref.shape
    barrier = pltpu.get_barrier_semaphore()
    for i in range(1, ring):
        pl.semaphore_signal(
            barrier, inc=1, device_id=(rec, lax.rem(me + i, ring)),
            device_id_type=pl.DeviceIdType.MESH,
        )
    loads = [
        pltpu.make_async_copy(
            x_hbm.at[pl.ds(c * n, n)], x_ref.at[pl.ds(c * n, n)], x_sem.at[c]
        )
        for c in range(CHUNKS)
    ]
    place = {1: 0, 0: 1, 4: 2, 5: 7, 2: 8, 6: 9}
    weights = [
        pltpu.make_async_copy(
            w2_hbm.at[k],
            mid_ref if k == 3 else wt_ref.at[pl.ds(place[k] * c1, c1)],
            w_sem.at[k],
        )
        for k in range(taps)
    ]
    proj_load = pltpu.make_async_copy(proj_hbm, proj_ref, p_sem)
    loads[0].start()
    for w in weights:
        w.start()
    for load in loads[1:]:
        load.start()
    proj_load.start()
    w1p_ref[0:c0, :] = jnp.zeros((c0, c1), BF16)
    w1p_ref[c0:, :] = w1_ref[...].reshape(taps * c0, c1)
    bias = b1_ref[...]

    def sends(c):
        return [
            pltpu.make_async_remote_copy(
                src_ref=send_ref.at[lax.rem(me + i, ring), :, pl.ds(c * n, n)],
                dst_ref=got_ref.at[:, pl.ds(me * total_rows + c * n, n)],
                send_sem=send_sem.at[c, i - 1],
                recv_sem=recv_sem.at[c, i - 1],
                device_id=(rec, lax.rem(me + i, ring)),
                device_id_type=pl.DeviceIdType.MESH,
            )
            for i in range(1, ring)
        ]

    def chunk(c, _):
        start = pl.multiple_of(c * n, n)
        rows = pl.ds(start, n)
        pltpu.make_async_copy(x_hbm.at[rows], x_ref.at[rows], x_sem.at[c]).wait()
        first_layer(x_ref, rows, n, bias, w1p_ref, x0_ref, x1_ref, x2_ref, x3_ref, carry_ref)

        @pl.when(c == 0)
        def _():
            for w in weights:
                w.wait()

            def tap(k):
                if k == 3:
                    return mid_ref[...].astype(F32)
                return wt_ref[place[k] * c1 : (place[k] + 1) * c1, :].astype(F32)

            ends = tap(1) + tap(5)
            wt_ref[3 * c1 : 4 * c1, :] = (0.5 * (ends + tap(3))).astype(BF16)
            wt_ref[6 * c1 : 7 * c1, :] = (0.5 * (ends - tap(3))).astype(BF16)
            wt_ref[4 * c1 : 5 * c1, :] = (tap(0) + tap(2)).astype(BF16)
            wt_ref[5 * c1 : 6 * c1, :] = (tap(4) + tap(6)).astype(BF16)

        second_layer(n, b2_ref, wt_ref, x0_ref, x1_ref, x2_ref, x3_ref, part_ref, acc_ref)
        embedded = (acc_ref[...] * (0.25 / x2_ref.shape[0])).astype(BF16)

        @pl.when(c == 0)
        def _():
            proj_load.wait()
            pl.semaphore_wait(barrier, ring - 1)

        width = got_ref.shape[2]
        for j in range(3):
            mixed = dot(embedded, proj_ref[j])
            if j == 0:
                mixed = mixed * (LOG2E * HD**-0.5)
            mixed = mixed.astype(BF16)
            for peer in range(ring):
                send_ref[peer, j, rows, :] = mixed[:, peer * width : (peer + 1) * width]
        for copy in sends(c):
            copy.start()
        own = pl.ds(pl.multiple_of(me * total_rows + c * n, n), n)
        got_ref[:, own, :] = send_ref[me, :, rows, :]
        return 0

    lax.fori_loop(0, CHUNKS, chunk, 0)
    for c in range(CHUNKS):
        for copy in sends(c):
            copy.wait()
    attend(count_ref[0], got_ref.at[0], got_ref.at[1], got_ref.at[2], o_ref)


def shards(spectrogram, epoch_counts, conv_first, bias_first, conv_second, bias_second, projection):
    ring = lax.axis_size("head")
    x = spectrogram[0]
    rows, flat = x.shape
    n = rows // CHUNKS
    taps, c0, c1 = conv_first.shape
    width = conv_second.shape[2]
    pairs = flat // (8 * c0)
    group = width // ring
    vmem = pl.BlockSpec(memory_space=pltpu.VMEM)
    hbm = pl.BlockSpec(memory_space=pl.ANY)
    out = pl.pallas_call(
        functools.partial(body, ring),
        out_shape=jax.ShapeDtypeStruct((rows * ring, group), BF16),
        in_specs=[pl.BlockSpec(memory_space=pltpu.SMEM), hbm, vmem, vmem, hbm, vmem, hbm],
        out_specs=vmem,
        scratch_shapes=[
            pltpu.VMEM((rows, flat), BF16),
            pltpu.VMEM(((taps + 1) * c0, c1), BF16),
            pltpu.VMEM((10 * c1, width), BF16),
            pltpu.VMEM((c1, width), BF16),
            pltpu.VMEM((3, width, width), BF16),
            pltpu.VMEM((pairs + 1, n, 2 * c1), BF16),
            pltpu.VMEM((pairs + 1, n, 2 * c1), BF16),
            pltpu.VMEM((pairs, n, c1), BF16),
            pltpu.VMEM((pairs + 1, n, 2 * c1), BF16),
            pltpu.VMEM((3, n, c1), F32),
            pltpu.VMEM((4, PAIRS_STEP * n, c1), F32),
            pltpu.VMEM((n, width), F32),
            pltpu.VMEM((ring, 3, rows, group), BF16),
            pltpu.VMEM((3, rows * ring, group), BF16),
            pltpu.SemaphoreType.DMA((CHUNKS,)),
            pltpu.SemaphoreType.DMA((taps,)),
            pltpu.SemaphoreType.DMA,
            pltpu.SemaphoreType.DMA((CHUNKS, ring - 1)),
            pltpu.SemaphoreType.DMA((CHUNKS, ring - 1)),
        ],
        compiler_params=pltpu.CompilerParams(
            vmem_limit_bytes=56 * 1024 * 1024, collective_id=0, has_side_effects=True
        ),
        name="stem_attention",
    )(
        epoch_counts, x, conv_first, bias_first.reshape(1, -1), conv_second,
        bias_second.reshape(1, -1), jnp.transpose(projection, (1, 0, 2)),
    )
    return out[None]


def solution(mesh):
    return jax.shard_map(
        shards,
        mesh=mesh,
        in_specs=(P("rec", "head", None), P("rec"), P(), P(), P(), P(), P()),
        out_specs=P("rec", None, "head"),
        check_vma=False,
    )
```

```python
import functools

import jax
import jax.numpy as jnp
from jax import lax
from jax.experimental import pallas as pl
from jax.experimental.pallas import tpu as pltpu
from jax.sharding import PartitionSpec as P

HD = 64
ROOT = 0.7978845608028654
CUBE = ROOT * 0.044715
LOG2E = 1.4426950408889634
CHUNKS = 3
FRAMES_STEP = 16
PAIRS_STEP = 16
Q_ROWS = 512
F32 = jnp.float32
BF16 = jnp.bfloat16


def gelu_twice(y):
    return y + y * jnp.tanh(y * (ROOT + CUBE * (y * y)))


def gelu_twice16(z):
    return z + z * jnp.tanh(z * (BF16(ROOT) + BF16(CUBE) * (z * z)))


def gelu_half(z):
    return z + z * jnp.tanh(z * (BF16(2 * ROOT) + BF16(8 * CUBE) * (z * z)))


def dot(a, b):
    return jnp.dot(a, b, preferred_element_type=F32)


def first_layer(x_ref, rows, n, bias, w1p_ref, x0_ref, x1_ref, x2_ref, x3_ref, carry_ref):
    c1 = w1p_ref.shape[1]
    lane = w1p_ref.shape[0] // 4
    frames = x_ref.shape[1] // lane
    blank = jnp.zeros((n, c1), BF16)
    x0_ref[0, :, c1:] = blank
    x1_ref[0, :, c1:] = blank
    carry_ref[...] = jnp.zeros_like(carry_ref)

    def emit(p, even0, odd0, even1, odd1):
        before1, before0, odd_before = carry_ref[0], carry_ref[1], carry_ref[2]
        x0_ref[p, :, :c1] = (before1 - even1).astype(BF16)
        x1_ref[p, :, :c1] = (even0 + even1).astype(BF16)
        x2_ref[p] = (even1 - even0).astype(BF16)
        x3_ref[p, :, :c1] = (before0 - even0).astype(BF16)
        x0_ref[p + 1, :, c1:] = (odd0 - odd1).astype(BF16)
        x1_ref[p + 1, :, c1:] = odd1.astype(BF16)
        x3_ref[p, :, c1:] = (odd_before - odd0).astype(BF16)
        carry_ref[0] = even1
        carry_ref[1] = even0
        carry_ref[2] = odd1

    def act(y):
        return gelu_half((y + bias).astype(BF16))

    def piece(t):
        lo, hi = max(t - 2, 0), min(t + 2, frames)
        weight = w1p_ref[(lo - t + 2) * lane : (hi - t + 2) * lane, :]
        return act(dot(x_ref[rows, lo * lane : hi * lane], weight))

    def window(t):
        return x_ref[rows, pl.ds(pl.multiple_of((t - 2) * lane, lane), 4 * lane)]

    def many(p, count):
        lhs = jnp.concatenate([window(4 * p + j) for j in range(4 * count)], axis=0)
        y = act(dot(lhs, w1p_ref[...]))
        for q in range(count):
            emit(p + q, *[y[(4 * q + j) * n : (4 * q + j + 1) * n] for j in range(4)])

    per = FRAMES_STEP // 4
    quads = frames // 4
    emit(0, *[piece(j) for j in range(4)])

    def step(i, _):
        many(1 + i * per, per)
        return 0

    loops = (quads - 2) // per
    lax.fori_loop(0, loops, step, 0)
    rest = quads - 1 - (1 + loops * per)
    if rest:
        many(1 + loops * per, rest)
    emit(quads - 1, *[piece(frames - 4 + j) for j in range(4)])
    x3_ref[quads, :, :c1] = carry_ref[1].astype(BF16)
    x3_ref[quads, :, c1:] = carry_ref[2].astype(BF16)


def second_layer(n, bias_ref, wt_ref, x0_ref, x1_ref, x2_ref, x3_ref, part_ref, acc_ref):
    c1 = x2_ref.shape[2]
    width = wt_ref.shape[1]
    acc_ref[...] = jnp.zeros_like(acc_ref)

    def step(i, _):
        def rows_of(make):
            return jnp.concatenate([make(i * PAIRS_STEP + g) for g in range(PAIRS_STEP)], axis=0)

        lhs0 = rows_of(lambda p: jnp.concatenate([x0_ref[p], x0_ref[p + 1, :, c1:]], axis=1))
        lhs1 = rows_of(lambda p: jnp.concatenate([x1_ref[p], x1_ref[p + 1, :, c1:]], axis=1))
        lhs2 = rows_of(lambda p: x2_ref[p])
        lhs3 = rows_of(
            lambda p: jnp.concatenate(
                [x3_ref[p + 1, :, :c1], x3_ref[p, :, c1:], x3_ref[p + 1, :, c1:]], axis=1
            )
        )
        for block in range(width // c1):
            cols = slice(block * c1, (block + 1) * c1)
            slot = (block % 2) * 2
            part_ref[slot] = dot(lhs1, wt_ref[3 * c1 : 6 * c1, cols]) + bias_ref[:, cols]
            part_ref[slot + 1] = dot(lhs2, wt_ref[6 * c1 : 7 * c1, cols])
            y0 = dot(lhs0, wt_ref[0 : 3 * c1, cols]) + (part_ref[slot] + part_ref[slot + 1])
            y1 = (part_ref[slot] - part_ref[slot + 1]) - dot(lhs3, wt_ref[7 * c1 : 10 * c1, cols])
            y = gelu_twice16(y0.astype(BF16)) + gelu_twice16(y1.astype(BF16))
            total = y[0:n].astype(F32)
            for g in range(1, PAIRS_STEP):
                total = total + y[g * n : (g + 1) * n].astype(F32)
            acc_ref[:, cols] += total
        return 0

    lax.fori_loop(0, x2_ref.shape[0] // PAIRS_STEP, step, 0)


def attend_parts(count, got_a, got_b, part_a, part_b, rows_all, o_ref, base_ref, top_ref, kv_ref, between):
    width = got_a.shape[2]
    zero = jnp.zeros((), F32)

    def slot_of(shape, offset, part, start):
        row = lax.broadcasted_iota(jnp.int32, shape, 0) + offset
        return lax.div(row, part) * rows_all + lax.rem(row, part) + start

    def lanes(n, head):
        lane = lax.broadcasted_iota(jnp.int32, (n, width), 1)
        at = HD if head == 0 else 0
        return (lane >= head * HD) & (lane < (head + 1) * HD), lane == at, at

    def prepare(got, part, start, off):
        n = got.shape[1]
        live = slot_of((n, width), 0, part, start) < count
        bias = jnp.where(live, zero, F32(-1e30))
        for head in range(2):
            mine, spare, _ = lanes(n, head)
            kv_ref[head, off : off + n, :] = jnp.where(
                mine, got[1].astype(F32), jnp.where(spare, bias, zero)
            ).astype(BF16)
            kv_ref[2 + head, off : off + n, :] = jnp.where(
                mine, got[2].astype(F32), jnp.where(spare, F32(1), zero)
            ).astype(BF16)

    def query(got, block, head):
        mine, spare, at = lanes(Q_ROWS, head)
        q = got[0, block * Q_ROWS : (block + 1) * Q_ROWS, :].astype(F32)
        return jnp.where(mine, q, jnp.where(spare, F32(1), zero)).astype(BF16), at

    def score(wide, head, lo, hi):
        return lax.dot_general(
            wide, kv_ref[head, lo:hi, :], (((1,), (1,)), ((), ())), preferred_element_type=F32
        )

    def gather(scores, top, head, lo, hi):
        return dot(jnp.exp2(scores - top).astype(BF16), kv_ref[2 + head, lo:hi, :])

    def finish(outs, block, part, start):
        lane = lax.broadcasted_iota(jnp.int32, (Q_ROWS, width), 1)
        out = jnp.where(lane < HD, outs[0], outs[1])
        live = slot_of((Q_ROWS, width), block * Q_ROWS, part, start) < count
        out = jnp.where(live, out, zero).astype(BF16)
        for k in range(Q_ROWS // part):
            at = (block * (Q_ROWS // part) + k) * rows_all + start
            o_ref[at : at + part, :] = out[k * part : (k + 1) * part]

    na, nb = got_a.shape[1], got_b.shape[1]
    prepare(got_a, part_a, 0, 0)
    for block in range(na // Q_ROWS):
        rows = slice(block * Q_ROWS, (block + 1) * Q_ROWS)
        for head in range(2):
            wide, _ = query(got_a, block, head)
            scores = score(wide, head, 0, na)
            top = jnp.max(scores, axis=1, keepdims=True)
            top_ref[head, rows, :] = jnp.broadcast_to(top, (Q_ROWS, width))
            base_ref[head, rows, :] = gather(scores, top, head, 0, na)
    between()
    prepare(got_b, part_b, part_a, na)
    for block in range(na // Q_ROWS):
        rows = slice(block * Q_ROWS, (block + 1) * Q_ROWS)
        outs = []
        for head in range(2):
            wide, at = query(got_a, block, head)
            scores = score(wide, head, na, na + nb)
            before = top_ref[head, rows, 0:1]
            top = jnp.maximum(before, jnp.max(scores, axis=1, keepdims=True))
            summed = base_ref[head, rows, :] * jnp.exp2(before - top)
            summed = summed + gather(scores, top, head, na, na + nb)
            outs.append(summed / summed[:, at : at + 1])
        finish(outs, block, part_a, 0)
    for block in range(nb // Q_ROWS):
        outs = []
        for head in range(2):
            wide, at = query(got_b, block, head)
            scores = score(wide, head, 0, na + nb)
            top = jnp.max(scores, axis=1, keepdims=True)
            summed = gather(scores, top, head, 0, na + nb)
            outs.append(summed / summed[:, at : at + 1])
        finish(outs, block, part_b, part_a)


def body(
    ring,
    count_ref, x_hbm, w1_ref, b1_ref, w2_hbm, b2_ref, proj_hbm,
    o_ref,
    x_ref, w1p_ref, wt_ref, mid_ref, proj_ref,
    x0_ref, x1_ref, x2_ref, x3_ref, carry_ref, part_ref, acc_ref, emb_ref,
    send_a, send_b, got_a, got_b, base_ref, top_ref, kv_ref,
    x_sem, w_sem, p_sem, send_sem, recv_sem,
):
    me = lax.axis_index("head")
    rec = lax.axis_index("rec")
    total_rows = x_ref.shape[0]
    n = total_rows // CHUNKS
    taps, c0, c1 = w1_ref.shape
    barrier = pltpu.get_barrier_semaphore()
    for i in range(1, ring):
        pl.semaphore_signal(
            barrier, inc=1, device_id=(rec, lax.rem(me + i, ring)),
            device_id_type=pl.DeviceIdType.MESH,
        )
    loads = [
        pltpu.make_async_copy(
            x_hbm.at[pl.ds(c * n, n)], x_ref.at[pl.ds(c * n, n)], x_sem.at[c]
        )
        for c in range(CHUNKS)
    ]
    place = {1: 0, 0: 1, 4: 2, 5: 7, 2: 8, 6: 9}
    weights = [
        pltpu.make_async_copy(
            w2_hbm.at[k],
            mid_ref if k == 3 else wt_ref.at[pl.ds(place[k] * c1, c1)],
            w_sem.at[k],
        )
        for k in range(taps)
    ]
    proj_load = pltpu.make_async_copy(proj_hbm, proj_ref, p_sem)
    loads[0].start()
    for w in weights:
        w.start()
    for load in loads[1:]:
        load.start()
    proj_load.start()
    w1p_ref[0:c0, :] = jnp.zeros((c0, c1), BF16)
    w1p_ref[c0:, :] = w1_ref[...].reshape(taps * c0, c1) * BF16(0.5)
    bias = b1_ref[...] * 0.5

    part_b = n
    part_a = total_rows - n
    groups = [(0, send_a, got_a, part_a, 0), (1, send_b, got_b, part_b, part_a)]

    def sends(group):
        g, src, dst, part, _ = group
        return [
            pltpu.make_async_remote_copy(
                src_ref=src.at[lax.rem(me + i, ring)],
                dst_ref=dst.at[:, pl.ds(pl.multiple_of(me * part, part), part)],
                send_sem=send_sem.at[g, i - 1],
                recv_sem=recv_sem.at[g, i - 1],
                device_id=(rec, lax.rem(me + i, ring)),
                device_id_type=pl.DeviceIdType.MESH,
            )
            for i in range(1, ring)
        ]

    def project(group):
        g, src, dst, part, start = group
        width = dst.shape[2]
        for j in range(3):
            mixed = dot(emb_ref[start : start + part, :], proj_ref[j])
            if j == 0:
                mixed = mixed * (LOG2E * HD**-0.5)
            mixed = mixed.astype(BF16)
            for peer in range(ring):
                src[peer, j] = mixed[:, peer * width : (peer + 1) * width]
        for copy in sends(group):
            copy.start()
        dst[:, pl.ds(pl.multiple_of(me * part, part), part), :] = src[me]

    def chunk(c, _):
        start = pl.multiple_of(c * n, n)
        rows = pl.ds(start, n)
        pltpu.make_async_copy(x_hbm.at[rows], x_ref.at[rows], x_sem.at[c]).wait()
        first_layer(x_ref, rows, n, bias, w1p_ref, x0_ref, x1_ref, x2_ref, x3_ref, carry_ref)

        @pl.when(c == 0)
        def _():
            for w in weights:
                w.wait()

            def tap(k):
                if k == 3:
                    return mid_ref[...].astype(F32)
                return wt_ref[place[k] * c1 : (place[k] + 1) * c1, :].astype(F32)

            ends = tap(1) + tap(5)
            wt_ref[3 * c1 : 4 * c1, :] = (0.5 * (ends + tap(3))).astype(BF16)
            wt_ref[6 * c1 : 7 * c1, :] = (0.5 * (ends - tap(3))).astype(BF16)
            wt_ref[4 * c1 : 5 * c1, :] = (tap(0) + tap(2)).astype(BF16)
            wt_ref[5 * c1 : 6 * c1, :] = (tap(4) + tap(6)).astype(BF16)

        second_layer(n, b2_ref, wt_ref, x0_ref, x1_ref, x2_ref, x3_ref, part_ref, acc_ref)
        emb_ref[rows, :] = (acc_ref[...] * (0.25 / x2_ref.shape[0])).astype(BF16)

        @pl.when(c == CHUNKS - 2)
        def _():
            proj_load.wait()
            pl.semaphore_wait(barrier, ring - 1)
            project(groups[0])

        return 0

    lax.fori_loop(0, CHUNKS, chunk, 0)
    project(groups[1])
    for copy in sends(groups[0]):
        copy.wait()

    def between():
        for copy in sends(groups[1]):
            copy.wait()

    attend_parts(
        count_ref[0], got_a, got_b, part_a, part_b, total_rows, o_ref, base_ref, top_ref, kv_ref, between
    )


def shards(spectrogram, epoch_counts, conv_first, bias_first, conv_second, bias_second, projection):
    ring = lax.axis_size("head")
    x = spectrogram[0]
    rows, flat = x.shape
    n = rows // CHUNKS
    taps, c0, c1 = conv_first.shape
    width = conv_second.shape[2]
    pairs = flat // (8 * c0)
    group = width // ring
    vmem = pl.BlockSpec(memory_space=pltpu.VMEM)
    hbm = pl.BlockSpec(memory_space=pl.ANY)
    out = pl.pallas_call(
        functools.partial(body, ring),
        out_shape=jax.ShapeDtypeStruct((rows * ring, group), BF16),
        in_specs=[pl.BlockSpec(memory_space=pltpu.SMEM), hbm, vmem, vmem, hbm, vmem, hbm],
        out_specs=vmem,
        scratch_shapes=[
            pltpu.VMEM((rows, flat), BF16),
            pltpu.VMEM(((taps + 1) * c0, c1), BF16),
            pltpu.VMEM((10 * c1, width), BF16),
            pltpu.VMEM((c1, width), BF16),
            pltpu.VMEM((3, width, width), BF16),
            pltpu.VMEM((pairs + 1, n, 2 * c1), BF16),
            pltpu.VMEM((pairs + 1, n, 2 * c1), BF16),
            pltpu.VMEM((pairs, n, c1), BF16),
            pltpu.VMEM((pairs + 1, n, 2 * c1), BF16),
            pltpu.VMEM((3, n, c1), BF16),
            pltpu.VMEM((4, PAIRS_STEP * n, c1), F32),
            pltpu.VMEM((n, width), F32),
            pltpu.VMEM((rows, width), BF16),
            pltpu.VMEM((ring, 3, rows - n, group), BF16),
            pltpu.VMEM((ring, 3, n, group), BF16),
            pltpu.VMEM((3, (rows - n) * ring, group), BF16),
            pltpu.VMEM((3, n * ring, group), BF16),
            pltpu.VMEM((2, (rows - n) * ring, group), F32),
            pltpu.VMEM((2, (rows - n) * ring, group), F32),
            pltpu.VMEM((4, rows * ring, group), BF16),
            pltpu.SemaphoreType.DMA((CHUNKS,)),
            pltpu.SemaphoreType.DMA((taps,)),
            pltpu.SemaphoreType.DMA,
            pltpu.SemaphoreType.DMA((2, ring - 1)),
            pltpu.SemaphoreType.DMA((2, ring - 1)),
        ],
        compiler_params=pltpu.CompilerParams(
            vmem_limit_bytes=56 * 1024 * 1024, collective_id=0, has_side_effects=True
        ),
        name="stem_attention",
    )(
        epoch_counts, x, conv_first, bias_first.reshape(1, -1), conv_second,
        bias_second.reshape(1, -1), jnp.transpose(projection, (1, 0, 2)),
    )
    return out[None]


def solution(mesh):
    return jax.shard_map(
        shards,
        mesh=mesh,
        in_specs=(P("rec", "head", None), P("rec"), P(), P(), P(), P(), P()),
        out_specs=P("rec", None, "head"),
        check_vma=False,
    )
```

```python
import functools

import jax
import jax.numpy as jnp
from jax import lax
from jax.experimental import pallas as pl
from jax.experimental.pallas import tpu as pltpu
from jax.sharding import PartitionSpec as P

HD = 64
ROOT = 0.7978845608028654
CUBE = ROOT * 0.044715
LOG2E = 1.4426950408889634
CHUNKS = 3
PARTS = 4
Q_ROWS = 512
F32 = jnp.float32
BF16 = jnp.bfloat16


def gelu_twice(y):
    return y + y * jnp.tanh(y * (ROOT + CUBE * (y * y)))


def gelu_twice16(z):
    return z + z * jnp.tanh(z * (BF16(ROOT) + BF16(CUBE) * (z * z)))


def gelu_half(z):
    return z + z * jnp.tanh(z * (BF16(2 * ROOT) + BF16(8 * CUBE) * (z * z)))


def dot(a, b):
    return jnp.dot(a, b, preferred_element_type=F32)


def first_parts(x_ref, start, n, bias, w1p_ref, xs, carry_ref):
    x0_ref, x1_ref, x2_ref, x3_ref = xs
    c1 = w1p_ref.shape[1]
    lane = w1p_ref.shape[0] // 4
    quads = x2_ref.shape[0]
    per = quads // PARTS

    def emit(p, even0, odd0, even1, odd1):
        before1, before0, odd_before = carry_ref[0], carry_ref[1], carry_ref[2]
        x0_ref[p, :, :c1] = before1 - even1
        x1_ref[p, :, :c1] = even0 + even1
        x2_ref[p] = even1 - even0
        x3_ref[p, :, :c1] = before0 - even0
        x0_ref[p + 1, :, c1:] = odd0 - odd1
        x1_ref[p + 1, :, c1:] = odd1
        x3_ref[p, :, c1:] = odd_before - odd0
        carry_ref[0] = even1
        carry_ref[1] = even0
        carry_ref[2] = odd1

    def part(k):
        if k == 0:
            blank = jnp.zeros((n, c1), BF16)
            x0_ref[0, :, c1:] = blank
            x1_ref[0, :, c1:] = blank
            carry_ref[...] = jnp.zeros_like(carry_ref)
        first = 4 * per * k
        lhs = jnp.concatenate(
            [x_ref[start : start + n, (first + j) * lane : (first + j + 4) * lane] for j in range(4 * per)],
            axis=0,
        )
        y = gelu_half((dot(lhs, w1p_ref[...]) + bias).astype(BF16))
        for q in range(per):
            emit(per * k + q, *[y[(4 * q + j) * n : (4 * q + j + 1) * n] for j in range(4)])
        if k == PARTS - 1:
            x3_ref[quads, :, :c1] = carry_ref[1]
            x3_ref[quads, :, c1:] = carry_ref[2]

    return part


def second_layer(n, bias_ref, wt_ref, xs, part_ref, emb_ref, start, weave):
    x0_ref, x1_ref, x2_ref, x3_ref = xs
    c1 = x2_ref.shape[2]
    pairs = x2_ref.shape[0]
    width = wt_ref.shape[1]

    def rows_of(make):
        return jnp.concatenate([make(p) for p in range(pairs)], axis=0)

    lhs0 = rows_of(lambda p: jnp.concatenate([x0_ref[p], x0_ref[p + 1, :, c1:]], axis=1))
    lhs1 = rows_of(lambda p: jnp.concatenate([x1_ref[p], x1_ref[p + 1, :, c1:]], axis=1))
    lhs2 = rows_of(lambda p: x2_ref[p])
    lhs3 = rows_of(
        lambda p: jnp.concatenate(
            [x3_ref[p + 1, :, :c1], x3_ref[p, :, c1:], x3_ref[p + 1, :, c1:]], axis=1
        )
    )
    for block in range(width // c1):
        cols = slice(block * c1, (block + 1) * c1)
        slot = (block % 2) * 2
        weave(block)
        part_ref[slot] = dot(lhs1, wt_ref[3 * c1 : 6 * c1, cols]) + bias_ref[:, cols]
        part_ref[slot + 1] = dot(lhs2, wt_ref[6 * c1 : 7 * c1, cols])
        y0 = dot(lhs0, wt_ref[0 : 3 * c1, cols]) + (part_ref[slot] + part_ref[slot + 1])
        y1 = (part_ref[slot] - part_ref[slot + 1]) - dot(lhs3, wt_ref[7 * c1 : 10 * c1, cols])
        y = gelu_twice16(y0.astype(BF16)) + gelu_twice16(y1.astype(BF16))
        total = y[0:n].astype(F32)
        for g in range(1, pairs):
            total = total + y[g * n : (g + 1) * n].astype(F32)
        emb_ref[start : start + n, cols] = (total * (0.25 / pairs)).astype(BF16)


def attend_parts(count, got_a, got_b, part_a, part_b, rows_all, o_ref, base_ref, top_ref, kv_ref, between):
    width = got_a.shape[2]
    zero = jnp.zeros((), F32)

    def slot_of(shape, offset, part, start):
        row = lax.broadcasted_iota(jnp.int32, shape, 0) + offset
        return lax.div(row, part) * rows_all + lax.rem(row, part) + start

    def lanes(n, head):
        lane = lax.broadcasted_iota(jnp.int32, (n, width), 1)
        at = HD if head == 0 else 0
        return (lane >= head * HD) & (lane < (head + 1) * HD), lane == at, at

    def prepare(got, part, start, off):
        n = got.shape[1]
        live = slot_of((n, width), 0, part, start) < count
        bias = jnp.where(live, zero, F32(-1e30))
        for head in range(2):
            mine, spare, _ = lanes(n, head)
            kv_ref[head, off : off + n, :] = jnp.where(
                mine, got[1].astype(F32), jnp.where(spare, bias, zero)
            ).astype(BF16)
            kv_ref[2 + head, off : off + n, :] = jnp.where(
                mine, got[2].astype(F32), jnp.where(spare, F32(1), zero)
            ).astype(BF16)

    def query(got, block, head):
        mine, spare, at = lanes(Q_ROWS, head)
        q = got[0, block * Q_ROWS : (block + 1) * Q_ROWS, :].astype(F32)
        return jnp.where(mine, q, jnp.where(spare, F32(1), zero)).astype(BF16), at

    def score(wide, head, lo, hi):
        return lax.dot_general(
            wide, kv_ref[head, lo:hi, :], (((1,), (1,)), ((), ())), preferred_element_type=F32
        )

    def gather(scores, top, head, lo, hi):
        return dot(jnp.exp2(scores - top).astype(BF16), kv_ref[2 + head, lo:hi, :])

    def finish(outs, block, part, start):
        lane = lax.broadcasted_iota(jnp.int32, (Q_ROWS, width), 1)
        out = jnp.where(lane < HD, outs[0], outs[1])
        out = out.astype(BF16)
        for k in range(Q_ROWS // part):
            at = (block * (Q_ROWS // part) + k) * rows_all + start
            o_ref[at : at + part, :] = out[k * part : (k + 1) * part]

    def ahead(tasks, scored, rest):
        current = scored(*tasks[0])
        for i, task in enumerate(tasks):
            upcoming = scored(*tasks[i + 1]) if i + 1 < len(tasks) else None
            rest(task, current)
            current = upcoming

    na, nb = got_a.shape[1], got_b.shape[1]
    prepare(got_a, part_a, 0, 0)

    def scored_first(block, head):
        return score(query(got_a, block, head)[0], head, 0, na)

    def rest_first(task, scores):
        block, head = task
        rows = slice(block * Q_ROWS, (block + 1) * Q_ROWS)
        top = jnp.max(scores, axis=1, keepdims=True)
        top_ref[head, rows, :] = jnp.broadcast_to(top, (Q_ROWS, width))
        base_ref[head, rows, :] = gather(scores, top, head, 0, na)

    ahead([(b, h) for b in range(na // Q_ROWS) for h in range(2)], scored_first, rest_first)
    between()
    prepare(got_b, part_b, part_a, na)
    kept = {}

    def scored_second(second, block, head):
        if second:
            return score(query(got_b, block, head)[0], head, 0, na + nb)
        return score(query(got_a, block, head)[0], head, na, na + nb)

    def rest_second(task, scores):
        second, block, head = task
        at = HD if head == 0 else 0
        rows = slice(block * Q_ROWS, (block + 1) * Q_ROWS)
        top = jnp.max(scores, axis=1, keepdims=True)
        if second:
            summed = gather(scores, top, head, 0, na + nb)
        else:
            before = top_ref[head, rows, 0:1]
            top = jnp.maximum(before, top)
            summed = base_ref[head, rows, :] * jnp.exp2(before - top)
            summed = summed + gather(scores, top, head, na, na + nb)
        kept[head] = summed / summed[:, at : at + 1]
        if head == 1:
            finish([kept[0], kept[1]], block, part_b if second else part_a, part_a if second else 0)

    ahead(
        [(g, b, h) for g, n in ((0, na), (1, nb)) for b in range(n // Q_ROWS) for h in range(2)],
        scored_second,
        rest_second,
    )


def body(
    ring,
    count_ref, x_hbm, w1_hbm, b1_hbm, w2_hbm, b2_hbm, proj_hbm,
    o_ref,
    x_ref, w1p_ref, b1_ref, b2_ref, wt_ref, mid_ref, proj_ref,
    xs_even, xs_odd, carry_ref, part_ref, emb_ref,
    send_a, send_b, got_a, got_b, base_ref, top_ref, kv_ref,
    x_sem, s_sem, w_sem, p_sem, send_sem, recv_sem,
):
    me = lax.axis_index("head")
    rec = lax.axis_index("rec")
    total_rows = x_ref.shape[0]
    n = total_rows // CHUNKS
    taps = w2_hbm.shape[0]
    wide, c1 = w1p_ref.shape
    c0 = wide // (taps + 1)
    barrier = pltpu.get_barrier_semaphore()
    for i in range(1, ring):
        pl.semaphore_signal(
            barrier, inc=1, device_id=(rec, lax.rem(me + i, ring)),
            device_id_type=pl.DeviceIdType.MESH,
        )
    loads = [
        pltpu.make_async_copy(
            x_hbm.at[pl.ds(c * n, n)],
            x_ref.at[pl.ds(c * n, n), pl.ds(4 * c0, x_hbm.shape[1])],
            x_sem.at[c],
        )
        for c in range(CHUNKS)
    ]
    place = {1: 0, 0: 1, 4: 2, 5: 7, 2: 8, 6: 9}
    weights = [
        pltpu.make_async_copy(
            w2_hbm.at[k],
            mid_ref if k == 3 else wt_ref.at[pl.ds(place[k] * c1, c1)],
            w_sem.at[k],
        )
        for k in range(taps)
    ]
    proj_load = pltpu.make_async_copy(proj_hbm, proj_ref, p_sem)
    small = [
        pltpu.make_async_copy(w1_hbm, w1p_ref.at[pl.ds(c0, taps * c0)], s_sem.at[0]),
        pltpu.make_async_copy(b1_hbm, b1_ref, s_sem.at[1]),
        pltpu.make_async_copy(b2_hbm, b2_ref, s_sem.at[2]),
    ]
    for load in small:
        load.start()
    loads[0].start()
    for w in weights:
        w.start()
    for load in loads[1:]:
        load.start()
    proj_load.start()
    x_ref[:, 0 : 4 * c0] = jnp.zeros((total_rows, 4 * c0), BF16)
    x_ref[:, 4 * c0 + x_hbm.shape[1] :] = jnp.zeros((total_rows, 2 * c0), BF16)
    w1p_ref[0:c0, :] = jnp.zeros((c0, c1), BF16)
    for load in small:
        load.wait()
    w1p_ref[c0:, :] = w1p_ref[c0:, :] * BF16(0.5)
    bias = b1_ref[...] * 0.5

    part_b = n
    part_a = total_rows - n
    groups = [(0, send_a, got_a, part_a, 0), (1, send_b, got_b, part_b, part_a)]

    def sends(group):
        g, src, dst, part, _ = group
        return [
            pltpu.make_async_remote_copy(
                src_ref=src.at[lax.rem(me + i, ring)],
                dst_ref=dst.at[:, pl.ds(pl.multiple_of(me * part, part), part)],
                send_sem=send_sem.at[g, i - 1],
                recv_sem=recv_sem.at[g, i - 1],
                device_id=(rec, lax.rem(me + i, ring)),
                device_id_type=pl.DeviceIdType.MESH,
            )
            for i in range(1, ring)
        ]

    def project(group):
        g, src, dst, part, start = group
        width = dst.shape[2]
        for j in range(3):
            mixed = dot(emb_ref[start : start + part, :], proj_ref[j])
            if j == 0:
                mixed = mixed * (LOG2E * HD**-0.5)
            mixed = mixed.astype(BF16)
            for peer in range(ring):
                src[peer, j] = mixed[:, peer * width : (peer + 1) * width]
        for copy in sends(group):
            copy.start()
        dst[:, pl.ds(pl.multiple_of(me * part, part), part), :] = src[me]

    xs = (xs_even, xs_odd)

    def parts_of(c):
        return first_parts(x_ref, c * n, n, bias, w1p_ref, xs[c % 2], carry_ref)

    loads[0].wait()
    for k in range(PARTS):
        parts_of(0)(k)
    for w in weights:
        w.wait()

    def tap(k):
        if k == 3:
            return mid_ref[...]
        return wt_ref[place[k] * c1 : (place[k] + 1) * c1, :]

    wt_ref[4 * c1 : 5 * c1, :] = tap(0) + tap(2)
    wt_ref[5 * c1 : 6 * c1, :] = tap(4) + tap(6)
    ends = tap(1).astype(F32) + tap(5).astype(F32)
    middle = tap(3).astype(F32)
    wt_ref[3 * c1 : 4 * c1, :] = (0.5 * (ends + middle)).astype(BF16)
    wt_ref[6 * c1 : 7 * c1, :] = (0.5 * (ends - middle)).astype(BF16)
    for c in range(CHUNKS):
        if c + 1 < CHUNKS:
            loads[c + 1].wait()
            weave = parts_of(c + 1)
        else:
            weave = lambda k: None
        second_layer(n, b2_ref, wt_ref, xs[c % 2], part_ref, emb_ref, c * n, weave)
        if c == CHUNKS - 2:
            proj_load.wait()
            pl.semaphore_wait(barrier, ring - 1)
            project(groups[0])
    project(groups[1])
    for copy in sends(groups[0]):
        copy.wait()

    def between():
        for copy in sends(groups[1]):
            copy.wait()

    attend_parts(
        count_ref[0], got_a, got_b, part_a, part_b, total_rows, o_ref, base_ref, top_ref, kv_ref, between
    )


def shards(spectrogram, epoch_counts, conv_first, bias_first, conv_second, bias_second, projection):
    ring = lax.axis_size("head")
    x = spectrogram[0]
    rows, flat = x.shape
    n = rows // CHUNKS
    taps, c0, c1 = conv_first.shape
    width = conv_second.shape[2]
    pairs = flat // (8 * c0)
    group = width // ring
    stage = (
        pltpu.VMEM((pairs + 1, n, 2 * c1), BF16),
        pltpu.VMEM((pairs + 1, n, 2 * c1), BF16),
        pltpu.VMEM((pairs, n, c1), BF16),
        pltpu.VMEM((pairs + 1, n, 2 * c1), BF16),
    )
    vmem = pl.BlockSpec(memory_space=pltpu.VMEM)
    hbm = pl.BlockSpec(memory_space=pltpu.HBM)
    out = pl.pallas_call(
        functools.partial(body, ring),
        out_shape=jax.ShapeDtypeStruct((rows * ring, group), BF16),
        in_specs=[pl.BlockSpec(memory_space=pltpu.SMEM), hbm, hbm, hbm, hbm, hbm, hbm],
        out_specs=vmem,
        scratch_shapes=[
            pltpu.VMEM((rows, flat + 6 * c0), BF16),
            pltpu.VMEM(((taps + 1) * c0, c1), BF16),
            pltpu.VMEM((1, c1), F32),
            pltpu.VMEM((1, width), F32),
            pltpu.VMEM((10 * c1, width), BF16),
            pltpu.VMEM((c1, width), BF16),
            pltpu.VMEM((3, width, width), BF16),
            stage,
            stage,
            pltpu.VMEM((3, n, c1), BF16),
            pltpu.VMEM((4, pairs * n, c1), F32),
            pltpu.VMEM((rows, width), BF16),
            pltpu.VMEM((ring, 3, rows - n, group), BF16),
            pltpu.VMEM((ring, 3, n, group), BF16),
            pltpu.VMEM((3, (rows - n) * ring, group), BF16),
            pltpu.VMEM((3, n * ring, group), BF16),
            pltpu.VMEM((2, (rows - n) * ring, group), F32),
            pltpu.VMEM((2, (rows - n) * ring, group), F32),
            pltpu.VMEM((4, rows * ring, group), BF16),
            pltpu.SemaphoreType.DMA((CHUNKS,)),
            pltpu.SemaphoreType.DMA((3,)),
            pltpu.SemaphoreType.DMA((taps,)),
            pltpu.SemaphoreType.DMA,
            pltpu.SemaphoreType.DMA((2, ring - 1)),
            pltpu.SemaphoreType.DMA((2, ring - 1)),
        ],
        compiler_params=pltpu.CompilerParams(
            vmem_limit_bytes=52 * 1024 * 1024, collective_id=0, has_side_effects=True
        ),
        name="stem_attention",
    )(
        epoch_counts,
        *[
            pltpu.with_memory_space_constraint(v, pltpu.HBM)
            for v in (
                x, conv_first.reshape(taps * c0, c1), bias_first.reshape(1, -1), conv_second,
                bias_second.reshape(1, -1), jnp.transpose(projection, (1, 0, 2)),
            )
        ],
    )
    live = jnp.arange(out.shape[0], dtype=jnp.int32) < epoch_counts[0]
    return jnp.where(live[:, None], out, jnp.zeros_like(out))[None]


def solution(mesh):
    return jax.shard_map(
        shards,
        mesh=mesh,
        in_specs=(P("rec", "head", None), P("rec"), P(), P(), P(), P(), P()),
        out_specs=P("rec", None, "head"),
        check_vma=False,
    )
```

```python
import functools

import jax
import jax.numpy as jnp
from jax import lax
from jax.experimental import pallas as pl
from jax.experimental.pallas import tpu as pltpu
from jax.sharding import PartitionSpec as P

HD = 64
ROOT = 0.7978845608028654
CUBE = ROOT * 0.044715
LOG2E = 1.4426950408889634
CHUNKS = 3
PARTS = 4
Q_ROWS = 512
F32 = jnp.float32
BF16 = jnp.bfloat16


def gelu_twice(y):
    return y + y * jnp.tanh(y * (ROOT + CUBE * (y * y)))


def gelu_twice16(z):
    return z + z * jnp.tanh(z * (BF16(ROOT) + BF16(CUBE) * (z * z)))


def gelu_half(z):
    return z + z * jnp.tanh(z * (BF16(2 * ROOT) + BF16(8 * CUBE) * (z * z)))


def dot(a, b):
    return jnp.dot(a, b, preferred_element_type=F32)


def first_parts(x_ref, start, n, bias, w1p_ref, xs, carry_ref):
    x0_ref, x1_ref, x2_ref, x3_ref = xs
    c1 = w1p_ref.shape[1]
    lane = w1p_ref.shape[0] // 4
    quads = x2_ref.shape[0]
    per = quads // PARTS

    def emit(p, even0, odd0, even1, odd1):
        before1, before0, odd_before = carry_ref[0], carry_ref[1], carry_ref[2]
        x0_ref[p, :, :c1] = before1 - even1
        x1_ref[p, :, :c1] = even0 + even1
        x2_ref[p] = even1 - even0
        x3_ref[p, :, :c1] = before0 - even0
        x0_ref[p + 1, :, c1:] = odd0 - odd1
        x1_ref[p + 1, :, c1:] = odd1
        x3_ref[p, :, c1:] = odd_before - odd0
        carry_ref[0] = even1
        carry_ref[1] = even0
        carry_ref[2] = odd1

    def part(k):
        if k == 0:
            blank = jnp.zeros((n, c1), BF16)
            x0_ref[0, :, c1:] = blank
            x1_ref[0, :, c1:] = blank
            carry_ref[...] = jnp.zeros_like(carry_ref)
        first = 4 * per * k
        lhs = jnp.concatenate(
            [x_ref[start : start + n, (first + j) * lane : (first + j + 4) * lane] for j in range(4 * per)],
            axis=0,
        )
        y = gelu_half((dot(lhs, w1p_ref[...]) + bias).astype(BF16))
        for q in range(per):
            emit(per * k + q, *[y[(4 * q + j) * n : (4 * q + j + 1) * n] for j in range(4)])
        if k == PARTS - 1:
            x3_ref[quads, :, :c1] = carry_ref[1]
            x3_ref[quads, :, c1:] = carry_ref[2]

    return part


def second_layer(n, bias_ref, wt_ref, xs, part_ref, emb_ref, start, weave):
    x0_ref, x1_ref, x2_ref, x3_ref = xs
    c1 = x2_ref.shape[2]
    pairs = x2_ref.shape[0]
    width = wt_ref.shape[1]

    def rows_of(make):
        return jnp.concatenate([make(p) for p in range(pairs)], axis=0)

    lhs0 = rows_of(lambda p: jnp.concatenate([x0_ref[p], x0_ref[p + 1, :, c1:]], axis=1))
    lhs1 = rows_of(lambda p: jnp.concatenate([x1_ref[p], x1_ref[p + 1, :, c1:]], axis=1))
    lhs2 = rows_of(lambda p: x2_ref[p])
    lhs3 = rows_of(
        lambda p: jnp.concatenate(
            [x3_ref[p + 1, :, :c1], x3_ref[p, :, c1:], x3_ref[p + 1, :, c1:]], axis=1
        )
    )
    blocks = width // c1

    def products(block):
        cols = slice(block * c1, (block + 1) * c1)
        slot = (block % 2) * 2
        part_ref[slot] = dot(lhs1, wt_ref[3 * c1 : 6 * c1, cols]) + bias_ref[:, cols]
        part_ref[slot + 1] = dot(lhs2, wt_ref[6 * c1 : 7 * c1, cols])
        y0 = dot(lhs0, wt_ref[0 : 3 * c1, cols]) + (part_ref[slot] + part_ref[slot + 1])
        y1 = (part_ref[slot] - part_ref[slot + 1]) - dot(lhs3, wt_ref[7 * c1 : 10 * c1, cols])
        return y0.astype(BF16), y1.astype(BF16)

    weave(0)
    current = products(0)
    for block in range(blocks):
        upcoming = None
        if block + 1 < blocks:
            weave(block + 1)
            upcoming = products(block + 1)
        y = gelu_twice16(current[0]) + gelu_twice16(current[1])
        total = y[0:n].astype(F32)
        for g in range(1, pairs):
            total = total + y[g * n : (g + 1) * n].astype(F32)
        cols = slice(block * c1, (block + 1) * c1)
        emb_ref[start : start + n, cols] = (total * (0.25 / pairs)).astype(BF16)
        current = upcoming


def attend_parts(count, got_a, got_b, part_a, part_b, rows_all, o_ref, base_ref, top_ref, kv_ref, between):
    width = got_a.shape[2]
    zero = jnp.zeros((), F32)

    def slot_of(shape, offset, part, start):
        row = lax.broadcasted_iota(jnp.int32, shape, 0) + offset
        return lax.div(row, part) * rows_all + lax.rem(row, part) + start

    def lanes(n, head):
        lane = lax.broadcasted_iota(jnp.int32, (n, width), 1)
        at = HD if head == 0 else 0
        return (lane >= head * HD) & (lane < (head + 1) * HD), lane == at, at

    def prepare(got, part, start, off):
        n = got.shape[1]
        live = slot_of((n, width), 0, part, start) < count
        bias = jnp.where(live, zero, F32(-1e30))
        for head in range(2):
            mine, spare, _ = lanes(n, head)
            kv_ref[head, off : off + n, :] = jnp.where(
                mine, got[1].astype(F32), jnp.where(spare, bias, zero)
            ).astype(BF16)
            kv_ref[2 + head, off : off + n, :] = jnp.where(
                mine, got[2].astype(F32), jnp.where(spare, F32(1), zero)
            ).astype(BF16)

    def query(got, block, head):
        mine, spare, at = lanes(Q_ROWS, head)
        q = got[0, block * Q_ROWS : (block + 1) * Q_ROWS, :].astype(F32)
        return jnp.where(mine, q, jnp.where(spare, F32(1), zero)).astype(BF16), at

    def score(wide, head, lo, hi):
        return lax.dot_general(
            wide, kv_ref[head, lo:hi, :], (((1,), (1,)), ((), ())), preferred_element_type=F32
        )

    def gather(scores, top, head, lo, hi):
        return dot(jnp.exp2(scores - top).astype(BF16), kv_ref[2 + head, lo:hi, :])

    def finish(outs, block, part, start):
        lane = lax.broadcasted_iota(jnp.int32, (Q_ROWS, width), 1)
        out = jnp.where(lane < HD, outs[0], outs[1])
        out = out.astype(BF16)
        for k in range(Q_ROWS // part):
            at = (block * (Q_ROWS // part) + k) * rows_all + start
            o_ref[at : at + part, :] = out[k * part : (k + 1) * part]

    def ahead(tasks, scored, rest):
        current = scored(*tasks[0])
        for i, task in enumerate(tasks):
            upcoming = scored(*tasks[i + 1]) if i + 1 < len(tasks) else None
            rest(task, current)
            current = upcoming

    na, nb = got_a.shape[1], got_b.shape[1]
    prepare(got_a, part_a, 0, 0)

    def scored_first(block, head):
        return score(query(got_a, block, head)[0], head, 0, na)

    def rest_first(task, scores):
        block, head = task
        rows = slice(block * Q_ROWS, (block + 1) * Q_ROWS)
        top = jnp.max(scores, axis=1, keepdims=True)
        top_ref[head, rows, :] = jnp.broadcast_to(top, (Q_ROWS, width))
        base_ref[head, rows, :] = gather(scores, top, head, 0, na)

    ahead([(b, h) for b in range(na // Q_ROWS) for h in range(2)], scored_first, rest_first)
    between()
    prepare(got_b, part_b, part_a, na)
    kept = {}

    def scored_second(second, block, head):
        if second:
            return score(query(got_b, block, head)[0], head, 0, na + nb)
        return score(query(got_a, block, head)[0], head, na, na + nb)

    def rest_second(task, scores):
        second, block, head = task
        at = HD if head == 0 else 0
        rows = slice(block * Q_ROWS, (block + 1) * Q_ROWS)
        top = jnp.max(scores, axis=1, keepdims=True)
        if second:
            summed = gather(scores, top, head, 0, na + nb)
        else:
            before = top_ref[head, rows, 0:1]
            top = jnp.maximum(before, top)
            summed = base_ref[head, rows, :] * jnp.exp2(before - top)
            summed = summed + gather(scores, top, head, na, na + nb)
        kept[head] = summed / summed[:, at : at + 1]
        if head == 1:
            finish([kept[0], kept[1]], block, part_b if second else part_a, part_a if second else 0)

    ahead(
        [(g, b, h) for g, n in ((0, na), (1, nb)) for b in range(n // Q_ROWS) for h in range(2)],
        scored_second,
        rest_second,
    )


def body(
    ring,
    count_ref, x_hbm, w1_hbm, b1_hbm, w2_hbm, b2_hbm, proj_hbm,
    o_ref,
    x_ref, w1p_ref, b1_ref, b2_ref, wt_ref, mid_ref, proj_ref,
    xs_even, xs_odd, carry_ref, part_ref, emb_ref,
    send_a, send_b, got_a, got_b, base_ref, top_ref, kv_ref,
    x_sem, s_sem, w_sem, p_sem, send_sem, recv_sem,
):
    me = lax.axis_index("head")
    rec = lax.axis_index("rec")
    total_rows = x_ref.shape[0]
    n = total_rows // CHUNKS
    taps = w2_hbm.shape[0]
    wide, c1 = w1p_ref.shape
    c0 = wide // (taps + 1)
    barrier = pltpu.get_barrier_semaphore()
    for i in range(1, ring):
        pl.semaphore_signal(
            barrier, inc=1, device_id=(rec, lax.rem(me + i, ring)),
            device_id_type=pl.DeviceIdType.MESH,
        )
    loads = [
        pltpu.make_async_copy(
            x_hbm.at[pl.ds(c * n, n)],
            x_ref.at[pl.ds(c * n, n), pl.ds(4 * c0, x_hbm.shape[1])],
            x_sem.at[c],
        )
        for c in range(CHUNKS)
    ]
    place = {1: 0, 0: 1, 4: 2, 5: 7, 2: 8, 6: 9}
    weights = [
        pltpu.make_async_copy(
            w2_hbm.at[k],
            mid_ref if k == 3 else wt_ref.at[pl.ds(place[k] * c1, c1)],
            w_sem.at[k],
        )
        for k in range(taps)
    ]
    proj_load = pltpu.make_async_copy(proj_hbm, proj_ref, p_sem)
    small = [
        pltpu.make_async_copy(w1_hbm, w1p_ref.at[pl.ds(c0, taps * c0)], s_sem.at[0]),
        pltpu.make_async_copy(b1_hbm, b1_ref, s_sem.at[1]),
        pltpu.make_async_copy(b2_hbm, b2_ref, s_sem.at[2]),
    ]
    for load in small:
        load.start()
    loads[0].start()
    for w in weights:
        w.start()
    x_ref[:, 0 : 4 * c0] = jnp.zeros((total_rows, 4 * c0), BF16)
    x_ref[:, 4 * c0 + x_hbm.shape[1] :] = jnp.zeros((total_rows, 2 * c0), BF16)
    w1p_ref[0:c0, :] = jnp.zeros((c0, c1), BF16)
    for load in small:
        load.wait()
    w1p_ref[c0:, :] = w1p_ref[c0:, :] * BF16(0.5)
    bias = b1_ref[...] * 0.5

    part_b = n
    part_a = total_rows - n
    groups = [(0, send_a, got_a, part_a, 0), (1, send_b, got_b, part_b, part_a)]

    def sends(group):
        g, src, dst, part, _ = group
        return [
            pltpu.make_async_remote_copy(
                src_ref=src.at[lax.rem(me + i, ring)],
                dst_ref=dst.at[:, pl.ds(pl.multiple_of(me * part, part), part)],
                send_sem=send_sem.at[g, i - 1],
                recv_sem=recv_sem.at[g, i - 1],
                device_id=(rec, lax.rem(me + i, ring)),
                device_id_type=pl.DeviceIdType.MESH,
            )
            for i in range(1, ring)
        ]

    def project(group):
        g, src, dst, part, start = group
        width = dst.shape[2]
        for j in range(3):
            mixed = dot(emb_ref[start : start + part, :], proj_ref[j])
            if j == 0:
                mixed = mixed * (LOG2E * HD**-0.5)
            mixed = mixed.astype(BF16)
            for peer in range(ring):
                src[peer, j] = mixed[:, peer * width : (peer + 1) * width]
        for copy in sends(group):
            copy.start()
        dst[:, pl.ds(pl.multiple_of(me * part, part), part), :] = src[me]

    xs = (xs_even, xs_odd)

    def parts_of(c):
        return first_parts(x_ref, c * n, n, bias, w1p_ref, xs[c % 2], carry_ref)

    loads[0].wait()
    for load in loads[1:]:
        load.start()
    for k in range(PARTS):
        parts_of(0)(k)
    for w in weights:
        w.wait()
    proj_load.start()

    def tap(k):
        if k == 3:
            return mid_ref[...]
        return wt_ref[place[k] * c1 : (place[k] + 1) * c1, :]

    wt_ref[4 * c1 : 5 * c1, :] = tap(0) + tap(2)
    wt_ref[5 * c1 : 6 * c1, :] = tap(4) + tap(6)
    ends = tap(1).astype(F32) + tap(5).astype(F32)
    middle = tap(3).astype(F32)
    wt_ref[3 * c1 : 4 * c1, :] = (0.5 * (ends + middle)).astype(BF16)
    wt_ref[6 * c1 : 7 * c1, :] = (0.5 * (ends - middle)).astype(BF16)
    for c in range(CHUNKS):
        if c + 1 < CHUNKS:
            loads[c + 1].wait()
            weave = parts_of(c + 1)
        else:
            weave = lambda k: None
        second_layer(n, b2_ref, wt_ref, xs[c % 2], part_ref, emb_ref, c * n, weave)
        if c == CHUNKS - 2:
            proj_load.wait()
            pl.semaphore_wait(barrier, ring - 1)
            project(groups[0])
    project(groups[1])
    for copy in sends(groups[0]):
        copy.wait()

    def between():
        for copy in sends(groups[1]):
            copy.wait()

    attend_parts(
        count_ref[0], got_a, got_b, part_a, part_b, total_rows, o_ref, base_ref, top_ref, kv_ref, between
    )


def shards(spectrogram, epoch_counts, conv_first, bias_first, conv_second, bias_second, projection):
    ring = lax.axis_size("head")
    x = spectrogram[0]
    rows, flat = x.shape
    n = rows // CHUNKS
    taps, c0, c1 = conv_first.shape
    width = conv_second.shape[2]
    pairs = flat // (8 * c0)
    group = width // ring
    stage = (
        pltpu.VMEM((pairs + 1, n, 2 * c1), BF16),
        pltpu.VMEM((pairs + 1, n, 2 * c1), BF16),
        pltpu.VMEM((pairs, n, c1), BF16),
        pltpu.VMEM((pairs + 1, n, 2 * c1), BF16),
    )
    vmem = pl.BlockSpec(memory_space=pltpu.VMEM)
    hbm = pl.BlockSpec(memory_space=pltpu.HBM)
    out = pl.pallas_call(
        functools.partial(body, ring),
        out_shape=jax.ShapeDtypeStruct((rows * ring, group), BF16),
        in_specs=[pl.BlockSpec(memory_space=pltpu.SMEM), hbm, hbm, hbm, hbm, hbm, hbm],
        out_specs=vmem,
        scratch_shapes=[
            pltpu.VMEM((rows, flat + 6 * c0), BF16),
            pltpu.VMEM(((taps + 1) * c0, c1), BF16),
            pltpu.VMEM((1, c1), F32),
            pltpu.VMEM((1, width), F32),
            pltpu.VMEM((10 * c1, width), BF16),
            pltpu.VMEM((c1, width), BF16),
            pltpu.VMEM((3, width, width), BF16),
            stage,
            stage,
            pltpu.VMEM((3, n, c1), BF16),
            pltpu.VMEM((4, pairs * n, c1), F32),
            pltpu.VMEM((rows, width), BF16),
            pltpu.VMEM((ring, 3, rows - n, group), BF16),
            pltpu.VMEM((ring, 3, n, group), BF16),
            pltpu.VMEM((3, (rows - n) * ring, group), BF16),
            pltpu.VMEM((3, n * ring, group), BF16),
            pltpu.VMEM((2, (rows - n) * ring, group), F32),
            pltpu.VMEM((2, (rows - n) * ring, group), F32),
            pltpu.VMEM((4, rows * ring, group), BF16),
            pltpu.SemaphoreType.DMA((CHUNKS,)),
            pltpu.SemaphoreType.DMA((3,)),
            pltpu.SemaphoreType.DMA((taps,)),
            pltpu.SemaphoreType.DMA,
            pltpu.SemaphoreType.DMA((2, ring - 1)),
            pltpu.SemaphoreType.DMA((2, ring - 1)),
        ],
        compiler_params=pltpu.CompilerParams(
            vmem_limit_bytes=52 * 1024 * 1024, collective_id=0, has_side_effects=True
        ),
        name="stem_attention",
    )(
        epoch_counts,
        *[
            pltpu.with_memory_space_constraint(v, pltpu.HBM)
            for v in (
                x, conv_first.reshape(taps * c0, c1), bias_first.reshape(1, -1), conv_second,
                bias_second.reshape(1, -1), jnp.transpose(projection, (1, 0, 2)),
            )
        ],
    )
    live = jnp.arange(out.shape[0], dtype=jnp.int32) < epoch_counts[0]
    return jnp.where(live[:, None], out, jnp.zeros_like(out))[None]


def solution(mesh):
    return jax.shard_map(
        shards,
        mesh=mesh,
        in_specs=(P("rec", "head", None), P("rec"), P(), P(), P(), P(), P()),
        out_specs=P("rec", None, "head"),
        check_vma=False,
    )
```

```python
import functools

import jax
import jax.numpy as jnp
from jax import lax
from jax.experimental import pallas as pl
from jax.experimental.pallas import tpu as pltpu
from jax.sharding import PartitionSpec as P

HD = 64
ROOT = 0.7978845608028654
CUBE = ROOT * 0.044715
LOG2E = 1.4426950408889634
CHUNKS = 3
PARTS = 4
Q_ROWS = 512
F32 = jnp.float32
BF16 = jnp.bfloat16


def gelu_twice(y):
    return y + y * jnp.tanh(y * (ROOT + CUBE * (y * y)))


def gelu_twice16(z):
    return z + z * jnp.tanh(z * (BF16(ROOT) + BF16(CUBE) * (z * z)))


def gelu_half(z):
    return z + z * jnp.tanh(z * (BF16(2 * ROOT) + BF16(8 * CUBE) * (z * z)))


def dot(a, b):
    return jnp.dot(a, b, preferred_element_type=F32)


def first_parts(x_ref, start, n, bias, w1p_ref, xs, carry_ref):
    x0_ref, x1_ref, x2_ref, x3_ref = xs
    c1 = w1p_ref.shape[1]
    lane = w1p_ref.shape[0] // 4
    quads = x2_ref.shape[0]
    per = quads // PARTS

    def emit(p, even0, odd0, even1, odd1):
        before1, before0, odd_before = carry_ref[0], carry_ref[1], carry_ref[2]
        x0_ref[p, :, :c1] = before1 - even1
        x1_ref[p, :, :c1] = even0 + even1
        x2_ref[p] = even1 - even0
        x3_ref[p, :, :c1] = before0 - even0
        x0_ref[p + 1, :, c1:] = odd0 - odd1
        x1_ref[p + 1, :, c1:] = odd1
        x3_ref[p, :, c1:] = odd_before - odd0
        carry_ref[0] = even1
        carry_ref[1] = even0
        carry_ref[2] = odd1

    def part(k):
        if k == 0:
            blank = jnp.zeros((n, c1), BF16)
            x0_ref[0, :, c1:] = blank
            x1_ref[0, :, c1:] = blank
            carry_ref[...] = jnp.zeros_like(carry_ref)
        first = 4 * per * k
        lhs = jnp.concatenate(
            [x_ref[start : start + n, (first + j) * lane : (first + j + 4) * lane] for j in range(4 * per)],
            axis=0,
        )
        y = gelu_half((dot(lhs, w1p_ref[...]) + bias).astype(BF16))
        for q in range(per):
            emit(per * k + q, *[y[(4 * q + j) * n : (4 * q + j + 1) * n] for j in range(4)])
        if k == PARTS - 1:
            x3_ref[quads, :, :c1] = carry_ref[1]
            x3_ref[quads, :, c1:] = carry_ref[2]

    return part


def second_layer(n, bias_ref, wt_ref, xs, part_ref, emb_ref, start, weave):
    x0_ref, x1_ref, x2_ref, x3_ref = xs
    c1 = x2_ref.shape[2]
    pairs = x2_ref.shape[0]
    width = wt_ref.shape[1]

    def rows_of(make):
        return jnp.concatenate([make(p) for p in range(pairs)], axis=0)

    lhs0 = rows_of(lambda p: jnp.concatenate([x0_ref[p], x0_ref[p + 1, :, c1:]], axis=1))
    lhs1 = rows_of(lambda p: jnp.concatenate([x1_ref[p], x1_ref[p + 1, :, c1:]], axis=1))
    lhs2 = rows_of(lambda p: x2_ref[p])
    lhs3 = rows_of(
        lambda p: jnp.concatenate(
            [x3_ref[p + 1, :, :c1], x3_ref[p, :, c1:], x3_ref[p + 1, :, c1:]], axis=1
        )
    )
    blocks = width // c1

    def products(block):
        cols = slice(block * c1, (block + 1) * c1)
        slot = (block % 2) * 2
        part_ref[slot] = dot(lhs1, wt_ref[3 * c1 : 6 * c1, cols]) + bias_ref[:, cols]
        part_ref[slot + 1] = dot(lhs2, wt_ref[6 * c1 : 7 * c1, cols])
        y0 = dot(lhs0, wt_ref[0 : 3 * c1, cols]) + (part_ref[slot] + part_ref[slot + 1])
        y1 = (part_ref[slot] - part_ref[slot + 1]) - dot(lhs3, wt_ref[7 * c1 : 10 * c1, cols])
        return y0.astype(BF16), y1.astype(BF16)

    weave(0)
    current = products(0)
    for block in range(blocks):
        upcoming = None
        if block + 1 < blocks:
            weave(block + 1)
            upcoming = products(block + 1)
        y = gelu_twice16(current[0]) + gelu_twice16(current[1])
        total = y[0:n].astype(F32)
        for g in range(1, pairs):
            total = total + y[g * n : (g + 1) * n].astype(F32)
        cols = slice(block * c1, (block + 1) * c1)
        emb_ref[start : start + n, cols] = (total * (0.25 / pairs)).astype(BF16)
        current = upcoming


def attend_parts(count, got_a, got_b, part_a, part_b, rows_all, o_ref, base_ref, top_ref, kv_ref, between):
    width = got_a.shape[2]
    zero = jnp.zeros((), F32)

    def slot_of(shape, offset, part, start):
        row = lax.broadcasted_iota(jnp.int32, shape, 0) + offset
        return lax.div(row, part) * rows_all + lax.rem(row, part) + start

    def lanes(n, head):
        lane = lax.broadcasted_iota(jnp.int32, (n, width), 1)
        at = HD if head == 0 else 0
        return (lane >= head * HD) & (lane < (head + 1) * HD), lane == at, at

    def prepare(got, part, start, off):
        n = got.shape[1]
        live = slot_of((n, width), 0, part, start) < count
        bias = jnp.where(live, zero, F32(-1e30))
        for head in range(2):
            mine, spare, _ = lanes(n, head)
            kv_ref[head, off : off + n, :] = jnp.where(
                mine, got[1].astype(F32), jnp.where(spare, bias, zero)
            ).astype(BF16)
            kv_ref[2 + head, off : off + n, :] = jnp.where(
                mine, got[2].astype(F32), jnp.where(spare, F32(1), zero)
            ).astype(BF16)

    def query(got, block, head):
        mine, spare, at = lanes(Q_ROWS, head)
        q = got[0, block * Q_ROWS : (block + 1) * Q_ROWS, :].astype(F32)
        return jnp.where(mine, q, jnp.where(spare, F32(1), zero)).astype(BF16), at

    def score(wide, head, lo, hi):
        return lax.dot_general(
            wide, kv_ref[head, lo:hi, :], (((1,), (1,)), ((), ())), preferred_element_type=F32
        )

    def gather(scores, top, head, lo, hi):
        return dot(jnp.exp2(scores - top).astype(BF16), kv_ref[2 + head, lo:hi, :])

    def finish(outs, block, part, start):
        lane = lax.broadcasted_iota(jnp.int32, (Q_ROWS, width), 1)
        out = jnp.where(lane < HD, outs[0], outs[1])
        out = out.astype(BF16)
        for k in range(Q_ROWS // part):
            at = (block * (Q_ROWS // part) + k) * rows_all + start
            o_ref[at : at + part, :] = out[k * part : (k + 1) * part]

    def ahead(tasks, scored, rest):
        current = scored(*tasks[0])
        for i, task in enumerate(tasks):
            upcoming = scored(*tasks[i + 1]) if i + 1 < len(tasks) else None
            rest(task, current)
            current = upcoming

    na, nb = got_a.shape[1], got_b.shape[1]
    prepare(got_a, part_a, 0, 0)

    def scored_first(block, head):
        return score(query(got_a, block, head)[0], head, 0, na)

    def rest_first(task, scores):
        block, head = task
        rows = slice(block * Q_ROWS, (block + 1) * Q_ROWS)
        top = jnp.max(scores, axis=1, keepdims=True)
        top_ref[head, rows, :] = jnp.broadcast_to(top, (Q_ROWS, width))
        base_ref[head, rows, :] = gather(scores, top, head, 0, na)

    ahead([(b, h) for b in range(na // Q_ROWS) for h in range(2)], scored_first, rest_first)
    between()
    prepare(got_b, part_b, part_a, na)
    kept = {}

    def scored_second(second, block, head):
        if second:
            return score(query(got_b, block, head)[0], head, 0, na + nb)
        return score(query(got_a, block, head)[0], head, na, na + nb)

    def rest_second(task, scores):
        second, block, head = task
        at = HD if head == 0 else 0
        rows = slice(block * Q_ROWS, (block + 1) * Q_ROWS)
        top = jnp.max(scores, axis=1, keepdims=True)
        if second:
            summed = gather(scores, top, head, 0, na + nb)
        else:
            before = top_ref[head, rows, 0:1]
            top = jnp.maximum(before, top)
            summed = base_ref[head, rows, :] * jnp.exp2(before - top)
            summed = summed + gather(scores, top, head, na, na + nb)
        kept[head] = summed / summed[:, at : at + 1]
        if head == 1:
            finish([kept[0], kept[1]], block, part_b if second else part_a, part_a if second else 0)

    ahead(
        [(g, b, h) for g, n in ((0, na), (1, nb)) for b in range(n // Q_ROWS) for h in range(2)],
        scored_second,
        rest_second,
    )


def body(
    ring,
    count_ref, x_hbm, w1_hbm, b1_hbm, w2_hbm, b2_hbm, proj_hbm,
    o_ref,
    x_ref, w1p_ref, b1_ref, b2_ref, wt_ref, mid_ref, proj_ref,
    xs_even, xs_odd, carry_ref, part_ref, emb_ref,
    send_a, send_b, got_a, got_b, base_ref, top_ref, kv_ref,
    x_sem, s_sem, w_sem, p_sem, send_sem, recv_sem,
):
    me = lax.axis_index("head")
    rec = lax.axis_index("rec")
    total_rows = x_ref.shape[0]
    n = total_rows // CHUNKS
    taps = w2_hbm.shape[0]
    wide, c1 = w1p_ref.shape
    c0 = wide // (taps + 1)
    barrier = pltpu.get_barrier_semaphore()
    for i in range(1, ring):
        pl.semaphore_signal(
            barrier, inc=1, device_id=(rec, lax.rem(me + i, ring)),
            device_id_type=pl.DeviceIdType.MESH,
        )
    loads = [
        pltpu.make_async_copy(
            x_hbm.at[pl.ds(c * n, n)],
            x_ref.at[pl.ds(c * n, n), pl.ds(4 * c0, x_hbm.shape[1])],
            x_sem.at[c],
        )
        for c in range(CHUNKS)
    ]
    place = {1: 0, 0: 1, 4: 2, 5: 7, 2: 8, 6: 9}
    weights = [
        pltpu.make_async_copy(
            w2_hbm.at[k],
            mid_ref if k == 3 else wt_ref.at[pl.ds(place[k] * c1, c1)],
            w_sem.at[k],
        )
        for k in range(taps)
    ]
    proj_load = pltpu.make_async_copy(proj_hbm, proj_ref, p_sem)
    small = [
        pltpu.make_async_copy(w1_hbm, w1p_ref.at[pl.ds(c0, taps * c0)], s_sem.at[0]),
        pltpu.make_async_copy(b1_hbm, b1_ref, s_sem.at[1]),
        pltpu.make_async_copy(b2_hbm, b2_ref, s_sem.at[2]),
    ]
    for load in small:
        load.start()
    loads[0].start()
    for w in weights:
        w.start()
    x_ref[:, 0 : 4 * c0] = jnp.zeros((total_rows, 4 * c0), BF16)
    x_ref[:, 4 * c0 + x_hbm.shape[1] :] = jnp.zeros((total_rows, 2 * c0), BF16)
    w1p_ref[0:c0, :] = jnp.zeros((c0, c1), BF16)
    for load in small:
        load.wait()
    w1p_ref[c0:, :] = w1p_ref[c0:, :] * BF16(0.5)
    bias = b1_ref[...] * 0.5

    part_b = n
    part_a = total_rows - n
    groups = [(c, send_a, got_a, part_a, c * n) for c in range(CHUNKS - 1)]
    groups.append((CHUNKS - 1, send_b, got_b, part_b, 0))

    def sends(group):
        g, src, dst, part, off = group
        return [
            pltpu.make_async_remote_copy(
                src_ref=src.at[lax.rem(me + i, ring), :, pl.ds(off, n)],
                dst_ref=dst.at[:, pl.ds(pl.multiple_of(me * part + off, n), n)],
                send_sem=send_sem.at[g, i - 1],
                recv_sem=recv_sem.at[g, i - 1],
                device_id=(rec, lax.rem(me + i, ring)),
                device_id_type=pl.DeviceIdType.MESH,
            )
            for i in range(1, ring)
        ]

    def project(group):
        g, src, dst, part, off = group
        width = dst.shape[2]
        for j in range(3):
            mixed = dot(emb_ref[g * n : (g + 1) * n, :], proj_ref[j])
            if j == 0:
                mixed = mixed * (LOG2E * HD**-0.5)
            mixed = mixed.astype(BF16)
            for peer in range(ring):
                src[peer, j, off : off + n, :] = mixed[:, peer * width : (peer + 1) * width]
        for copy in sends(group):
            copy.start()
        dst[:, pl.ds(pl.multiple_of(me * part + off, n), n), :] = src[me, :, off : off + n, :]

    xs = (xs_even, xs_odd)

    def parts_of(c):
        return first_parts(x_ref, c * n, n, bias, w1p_ref, xs[c % 2], carry_ref)

    loads[0].wait()
    for load in loads[1:]:
        load.start()
    for k in range(PARTS):
        parts_of(0)(k)
    for w in weights:
        w.wait()
    proj_load.start()

    def tap(k):
        if k == 3:
            return mid_ref[...]
        return wt_ref[place[k] * c1 : (place[k] + 1) * c1, :]

    wt_ref[4 * c1 : 5 * c1, :] = tap(0) + tap(2)
    wt_ref[5 * c1 : 6 * c1, :] = tap(4) + tap(6)
    ends = tap(1).astype(F32) + tap(5).astype(F32)
    middle = tap(3).astype(F32)
    wt_ref[3 * c1 : 4 * c1, :] = (0.5 * (ends + middle)).astype(BF16)
    wt_ref[6 * c1 : 7 * c1, :] = (0.5 * (ends - middle)).astype(BF16)
    for c in range(CHUNKS):
        if c + 1 < CHUNKS:
            loads[c + 1].wait()
            weave = parts_of(c + 1)
        else:
            weave = lambda k: None
        second_layer(n, b2_ref, wt_ref, xs[c % 2], part_ref, emb_ref, c * n, weave)
        if c == 0:
            proj_load.wait()
            pl.semaphore_wait(barrier, ring - 1)
        project(groups[c])
    for group in groups[:-1]:
        for copy in sends(group):
            copy.wait()

    def between():
        for copy in sends(groups[-1]):
            copy.wait()

    attend_parts(
        count_ref[0], got_a, got_b, part_a, part_b, total_rows, o_ref, base_ref, top_ref, kv_ref, between
    )


def shards(spectrogram, epoch_counts, conv_first, bias_first, conv_second, bias_second, projection):
    ring = lax.axis_size("head")
    x = spectrogram[0]
    rows, flat = x.shape
    n = rows // CHUNKS
    taps, c0, c1 = conv_first.shape
    width = conv_second.shape[2]
    pairs = flat // (8 * c0)
    group = width // ring
    stage = (
        pltpu.VMEM((pairs + 1, n, 2 * c1), BF16),
        pltpu.VMEM((pairs + 1, n, 2 * c1), BF16),
        pltpu.VMEM((pairs, n, c1), BF16),
        pltpu.VMEM((pairs + 1, n, 2 * c1), BF16),
    )
    vmem = pl.BlockSpec(memory_space=pltpu.VMEM)
    hbm = pl.BlockSpec(memory_space=pltpu.HBM)
    out = pl.pallas_call(
        functools.partial(body, ring),
        out_shape=jax.ShapeDtypeStruct((rows * ring, group), BF16),
        in_specs=[pl.BlockSpec(memory_space=pltpu.SMEM), hbm, hbm, hbm, hbm, hbm, hbm],
        out_specs=vmem,
        scratch_shapes=[
            pltpu.VMEM((rows, flat + 6 * c0), BF16),
            pltpu.VMEM(((taps + 1) * c0, c1), BF16),
            pltpu.VMEM((1, c1), F32),
            pltpu.VMEM((1, width), F32),
            pltpu.VMEM((10 * c1, width), BF16),
            pltpu.VMEM((c1, width), BF16),
            pltpu.VMEM((3, width, width), BF16),
            stage,
            stage,
            pltpu.VMEM((3, n, c1), BF16),
            pltpu.VMEM((4, pairs * n, c1), F32),
            pltpu.VMEM((rows, width), BF16),
            pltpu.VMEM((ring, 3, rows - n, group), BF16),
            pltpu.VMEM((ring, 3, n, group), BF16),
            pltpu.VMEM((3, (rows - n) * ring, group), BF16),
            pltpu.VMEM((3, n * ring, group), BF16),
            pltpu.VMEM((2, (rows - n) * ring, group), F32),
            pltpu.VMEM((2, (rows - n) * ring, group), F32),
            pltpu.VMEM((4, rows * ring, group), BF16),
            pltpu.SemaphoreType.DMA((CHUNKS,)),
            pltpu.SemaphoreType.DMA((3,)),
            pltpu.SemaphoreType.DMA((taps,)),
            pltpu.SemaphoreType.DMA,
            pltpu.SemaphoreType.DMA((CHUNKS, ring - 1)),
            pltpu.SemaphoreType.DMA((CHUNKS, ring - 1)),
        ],
        compiler_params=pltpu.CompilerParams(
            vmem_limit_bytes=52 * 1024 * 1024, collective_id=0, has_side_effects=True
        ),
        name="stem_attention",
    )(
        epoch_counts,
        *[
            pltpu.with_memory_space_constraint(v, pltpu.HBM)
            for v in (
                x, conv_first.reshape(taps * c0, c1), bias_first.reshape(1, -1), conv_second,
                bias_second.reshape(1, -1), jnp.transpose(projection, (1, 0, 2)),
            )
        ],
    )
    live = jnp.arange(out.shape[0], dtype=jnp.int32) < epoch_counts[0]
    return jnp.where(live[:, None], out, jnp.zeros_like(out))[None]


def solution(mesh):
    return jax.shard_map(
        shards,
        mesh=mesh,
        in_specs=(P("rec", "head", None), P("rec"), P(), P(), P(), P(), P()),
        out_specs=P("rec", None, "head"),
        check_vma=False,
    )
```
